256 devices in a mesh: rows: 128 (over y, z, x), rep: 2 (over core).
Axes of the slice: x: 4, y: 4, z: 8, core: 2. Of those that a mesh axis runs over, the one named last changes fastest.
Arguments:
- grad_out: bfloat16 [16384, 1024], P('rows'), may hold values from -8 to 8
- w_self: bfloat16 [1024, 1024], replicated, may hold values from -0.1875 to 0.1875
- w_neigh: bfloat16 [1024, 1024], replicated, may hold values from -0.1875 to 0.1875
- adj_tiles: bfloat16 [128, 64, 128, 128], P('rows'), may hold values from -0.109375 to 0.109375
- tile_index: int32 [128, 64], P('rows'), may hold values from 0 to 127, as said below
- tile_count: int32 [128], P('rows'), may hold values from 4 to 64, as said below
- prompt_ids: int32 [16384], P('rows'), may hold values from 0 to 15
Outputs:
- input_grad: bfloat16 [16384, 1024], P('rows')
- prompt_grad: float32 [16, 1024], replicated
The draws below stay inside these ranges and needn't reach their ends.
Inputs may be any that keep to these rules, and one draw needn't show every extreme that they name: `tile_index`: each row holds 64 different tile numbers; only the first tile_count entries of a row are used. `tile_count`: some destination tile uses all 64 slots.
All inputs are finite; a program needn't handle non-finite values.
Results may differ from the reference program's by a relative error of at most 0.0041.
Values may be sent and summed in bfloat16 or wider, within the bound.
No kernel may reach another device: no remote copies, remote signals or barrier semaphores. Data moves between devices by JAX's collectives and lax.ppermute only.
A program may use at most 64 MiB of HBM per device.

```python
import math
import jax
import jax.numpy as jnp
from jax import lax

D = 1024
PROMPTS = 16
TILE = 128
NODES = 16384
TILES_ALL = 128
MAXT = 64


def draw_grad_out(key, part):
    base = jax.random.normal(jax.random.fold_in(key, 11), (NODES, D), jnp.float32)
    ramp = jnp.exp(jnp.linspace(math.log(0.5), math.log(1.5), NODES))[:, None]
    values = base * ramp
    return jnp.clip(values, -8.0, 8.0).astype(jnp.bfloat16)


def draw_tile_index(key, part):
    scores = jax.random.randint(jax.random.fold_in(key, 31), (TILES_ALL, TILES_ALL), 0, 2 ** 20)
    scores = scores * TILES_ALL + jnp.arange(TILES_ALL)[None, :]
    ordered = jnp.argsort(scores, axis=1, stable=True)
    return ordered[:, :MAXT].astype(jnp.int32)


def draw_tile_count(key, part):
    drawn = jax.random.randint(jax.random.fold_in(key, 21), (TILES_ALL,), 0, 64)
    counts = 4 + (MAXT - 4) * drawn * drawn // 3969
    chosen = jax.random.randint(jax.random.fold_in(key, 22), (), 0, TILES_ALL)
    counts = jnp.where(jnp.arange(TILES_ALL) == chosen, MAXT, counts)
    return counts.astype(jnp.int32)


def with_ends(result, own_key, low, top_value):
    extent = result.shape
    spot = [jax.random.randint(jax.random.fold_in(own_key, axis), (), 0, extent[axis]) for axis in range(len(extent))]
    result = result.at[tuple(spot)].set(low)
    longest = extent.index(max(extent))
    spot[longest] = (spot[longest] + 1) % extent[longest]
    return result.at[tuple(spot)].set(top_value)


def level_of(key, dims, shards, least, largest):
    def one(dim, parts):
        draws = jax.random.uniform(jax.random.fold_in(jax.random.fold_in(key, 6), dim), (parts,), jnp.float32, least / len(shards), largest / len(shards))
        return jnp.repeat(jnp.exp(draws), dims[dim] // parts).reshape((-1,) + (1,) * (len(dims) - dim - 1))

    factor_of = one(*shards[0])
    for cut in shards[1:]:
        factor_of = factor_of * one(*cut)
    return factor_of


def normal_values(own_key, shape, spread, most, pieces=(), held_as=jnp.bfloat16):
    values = jax.random.normal(own_key, shape, jnp.float32) * spread
    if len(pieces) > 0:
        values = level_of(own_key, shape, pieces, -0.22, 0.18) * values
    return jnp.clip(values, min=-most, max=most).astype(held_as)


def setup_inputs(seed: int = 0) -> dict:
    streams_of = jax.random.split(jax.random.key(seed), 8)
    grad_out = draw_grad_out(jax.random.fold_in(streams_of[7], 71), 0)
    w_self = normal_values(streams_of[1], (D, D), D ** -0.5, 0.1875)
    w_neigh = normal_values(streams_of[2], (D, D), D ** -0.5, 0.1875)
    adj_tiles = normal_values(streams_of[3], (TILES_ALL, MAXT, TILE, TILE), (TILE * MAXT // 3) ** -0.5, 0.109375, ((0, 128),))
    tile_index = draw_tile_index(jax.random.fold_in(streams_of[7], 71), 0)
    tile_count = draw_tile_count(jax.random.fold_in(streams_of[7], 71), 0)
    prompt_ids = with_ends(jax.random.randint(streams_of[6], (NODES,), 0, PROMPTS), jax.random.fold_in(streams_of[6], 1), 0, PROMPTS - 1).astype(jnp.int32)
    return {"grad_out": grad_out, "w_self": w_self, "w_neigh": w_neigh, "adj_tiles": adj_tiles, "tile_index": tile_index, "tile_count": tile_count, "prompt_ids": prompt_ids}


def reference(grad_out, w_self, w_neigh, adj_tiles, tile_index, tile_count, prompt_ids):
    tile_total = adj_tiles.shape[0]
    tile_size = adj_tiles.shape[2]
    width = grad_out.shape[1]
    node_blocks = grad_out.reshape(tile_total, tile_size, width)
    slot_ids = jnp.arange(adj_tiles.shape[1]).astype(jnp.int32)

    def one_tile(inputs):
        tile_set, tile_ids, used_count = inputs
        in_use = (slot_ids < used_count).astype(jnp.float32)
        sources = node_blocks[tile_ids.astype(jnp.int32)].astype(jnp.float32)
        weights_used = tile_set.astype(jnp.float32) * in_use[:, None, None]
        return jnp.einsum("kab,kbf->af", weights_used, sources, precision=lax.Precision.HIGHEST)

    aggregate = lax.map(one_tile, (adj_tiles, tile_index, tile_count))
    aggregate = aggregate.reshape(NODES, width).astype(jnp.bfloat16)
    full_grad = jnp.dot(grad_out, w_self.T, preferred_element_type=jnp.float32)
    full_grad = full_grad + jnp.dot(aggregate, w_neigh.T, preferred_element_type=jnp.float32)
    onehot = (prompt_ids[None, :] == jnp.arange(PROMPTS).astype(jnp.int32)[:, None]).astype(jnp.float32)
    prompt_grad = jnp.dot(onehot, full_grad, precision=lax.Precision.HIGHEST)
    return full_grad.astype(jnp.bfloat16), prompt_grad
```

```python
import jax
import jax.numpy as jnp
from jax import lax
from jax.experimental import pallas as pl
from jax.experimental.pallas import tpu as pltpu
from jax.sharding import PartitionSpec as P

PROMPTS = 16
NX, NY, NZ, NREP = 4, 4, 8, 2
GROUP = 4
AXES = ("rows", "rep")
ANY = pl.BlockSpec(memory_space=pl.ANY)
VMEM = pl.BlockSpec(memory_space=pltpu.VMEM)
SMEM = pl.BlockSpec(memory_space=pltpu.SMEM)


def pairs_of(role, step):
    pairs = []
    for y in range(NY):
        for z in range(NZ):
            for x in range(NX):
                for rep in range(NREP):
                    tx, ty, tz, trep = x, y, z, rep
                    if role == "rep":
                        trep = 1 - rep
                    elif role == "z":
                        tz = (z + step) % NZ
                    elif (role == "u") == (rep == 0):
                        tx = (x + step) % NX
                    else:
                        ty = (y + step) % NY
                    source = ((y * NZ + z) * NX + x) * NREP + rep
                    target = ((ty * NZ + tz) * NX + tx) * NREP + trep
                    pairs.append((source, target))
    return pairs


def send(value, role, step):
    return lax.ppermute(value, AXES, pairs_of(role, step))


def dot(a, b):
    return jnp.dot(a, b, preferred_element_type=jnp.float32)


def pack_kernel(first, info, low, high, out):
    half = info[0] * 64
    count = info[1]
    row = lax.broadcasted_iota(jnp.int32, (256, 128), 0)
    lane = lax.broadcasted_iota(jnp.int32, (256, 128), 1)
    wanted = jnp.where(lane < 64, half + lane, 64 + half + lane)
    pick = jnp.where(row == wanted, 1.0, 0.0).astype(jnp.bfloat16)
    out_lane = lax.broadcasted_iota(jnp.int32, (128, 128), 1)
    for i in range(low.shape[0]):
        slot = first + pl.program_id(0) * low.shape[0] + i
        both = jnp.concatenate([low[i], high[i]], axis=1)
        packed = dot(both, pick)
        last = jnp.where(out_lane < 64, slot, slot + 32)
        out[i] = jnp.where(last < count, packed, 0.0).astype(jnp.bfloat16)


def pack(adj, info, first):
    per = 4
    base = first // per
    grid_spec = pltpu.PrefetchScalarGridSpec(
        num_scalar_prefetch=1,
        grid=(16 // per,),
        in_specs=[
            pl.BlockSpec((per, 128, 128), lambda i, s: (base + i, 0, 0)),
            pl.BlockSpec((per, 128, 128), lambda i, s: (base + 32 // per + i, 0, 0)),
        ],
        out_specs=pl.BlockSpec((per, 128, 128), lambda i, s: (i, 0, 0)),
    )

    def body(info, low, high, out):
        pack_kernel(first, info, low, high, out)

    return pl.pallas_call(
        body,
        grid_spec=grid_spec,
        out_shape=jax.ShapeDtypeStruct((16, 128, 128), jnp.bfloat16),
        name="pack",
    )(info, adj, adj)


def split_kernel(info, grad, meta, *outs):
    start = pl.multiple_of(info[0] * 64, 64)
    for step in range(GROUP):
        u = lax.rem(info[2] + step, GROUP)
        lanes = pl.ds(pl.multiple_of(u * 256, 256), 256)
        outs[step][0:64, :] = grad[pl.ds(start, 64), lanes]
        outs[step][64:80, :] = meta[...]


def split(info, grad, meta):
    shape = jax.ShapeDtypeStruct((80, 256), jnp.bfloat16)
    return pl.pallas_call(
        split_kernel,
        in_specs=[SMEM, VMEM, VMEM],
        out_specs=[VMEM] * GROUP,
        out_shape=[shape] * GROUP,
        name="split",
    )(info, grad, meta)


def aggregate_kernel(where, ids, *refs):
    tiles = refs[0:8]
    chunks = refs[8:16]
    parts = refs[16:20]
    sums = refs[20]
    adj, table, adj_sem, table_sem = refs[21:]
    table_copies = []
    for i in range(8):
        copy = pltpu.make_async_copy(chunks[i], table.at[pl.ds(i * 16, 16)], table_sem.at[i])
        copy.start()
        table_copies.append(copy)
    adj_copies = []
    for i in range(8):
        copy = pltpu.make_async_copy(tiles[i], adj.at[pl.ds(i * 16, 16)], adj_sem.at[i])
        copy.start()
        adj_copies.append(copy)
    for copy in table_copies:
        copy.wait()
    total = jnp.zeros((PROMPTS, 256), jnp.float32)
    own = jnp.zeros((PROMPTS, 256), jnp.float32)
    rep = where[GROUP, 0]
    for d in range(GROUP):
        adj_copies[2 * d].wait()
        adj_copies[2 * d + 1].wait()
        acc = jnp.zeros((128, 256), jnp.float32)
        for q in range(16):
            p = 2 * q
            left = jnp.concatenate([adj[d * 32 + p], adj[d * 32 + p + 1]], axis=1)
            rows = [table[where[d, k]] for k in (p, p + 32, p + 1, p + 33)]
            acc = acc + dot(left, jnp.concatenate(rows, axis=0))
        parts[d][...] = acc
        number = lax.broadcasted_iota(jnp.int32, (PROMPTS, 128), 0)
        hot = jnp.where(ids[d : d + 1, :] == number, 1.0, 0.0).astype(jnp.bfloat16)
        high = acc.astype(jnp.bfloat16)
        low = (acc - high.astype(jnp.float32)).astype(jnp.bfloat16)
        total = total + dot(hot, high) + dot(hot, low)
        row = lax.broadcasted_iota(jnp.int32, (128, 1), 0)
        mine = (row // 64) == rep
        block = jnp.concatenate([table[d], table[d]], axis=0)
        block = jnp.where(mine, block.astype(jnp.float32), 0.0).astype(jnp.bfloat16)
        own = own + dot(hot, block)
    sums[0:PROMPTS, :] = own
    sums[PROMPTS : 2 * PROMPTS, :] = total


def aggregate(where, ids, tiles, chunks):
    part = jax.ShapeDtypeStruct((128, 256), jnp.float32)
    return pl.pallas_call(
        aggregate_kernel,
        in_specs=[SMEM, VMEM] + [ANY] * 16,
        out_specs=[VMEM] * 5,
        out_shape=[part] * 4 + [jax.ShapeDtypeStruct((2 * PROMPTS, 256), jnp.float32)],
        scratch_shapes=[
            pltpu.VMEM((128, 128, 128), jnp.bfloat16),
            pltpu.VMEM((128, 64, 256), jnp.bfloat16),
            pltpu.SemaphoreType.DMA((8,)),
            pltpu.SemaphoreType.DMA((8,)),
        ],
        compiler_params=pltpu.CompilerParams(vmem_limit_bytes=24 * 2**20),
        name="aggregate",
    )(where, ids, *tiles, *chunks)


def lanes_of(u, step):
    piece = lax.rem(u + step, GROUP)
    return pl.ds(pl.multiple_of(piece * 256, 256), 256)


ORDER = (0, 1, 3, 2)


def gather_pieces(info, mine, other, total):
    for i, step in enumerate(ORDER):
        total[:, lanes_of(info[2], step)] = mine[i][...]
    for i, step in enumerate(ORDER):
        lanes = lanes_of(info[3], step)
        total[:, lanes] = total[:, lanes] + other[i][...]


def finish_kernel(info, self_term, weight, *refs):
    mine, other, out, total = refs[0:4], refs[4:8], refs[8], refs[9]
    gather_pieces(info, mine, other, total)
    neighbours = total[...].astype(jnp.bfloat16)
    out[...] = (self_term[...] + dot(neighbours, weight[...])).astype(jnp.bfloat16)


def finish(info, self_term, weight, mine, other):
    return pl.pallas_call(
        finish_kernel,
        in_specs=[SMEM] + [VMEM] * 10,
        out_specs=VMEM,
        out_shape=jax.ShapeDtypeStruct((128, 1024), jnp.bfloat16),
        scratch_shapes=[pltpu.VMEM((128, 1024), jnp.float32)],
        compiler_params=pltpu.CompilerParams(vmem_limit_bytes=24 * 2**20),
        name="finish",
    )(info, self_term, weight, *mine, *other)


def dot_wide(a, b):
    high = a.astype(jnp.bfloat16)
    rest = a - high.astype(jnp.float32)
    middle = rest.astype(jnp.bfloat16)
    low = (rest - middle.astype(jnp.float32)).astype(jnp.bfloat16)
    product = dot(jnp.concatenate([high, middle, low], axis=0), b)
    return product[0:16] + product[16:32] + product[32:48]


def prompt_kernel(info, weight_self, weight_neigh, *refs):
    mine, other, out, total = refs[0:4], refs[4:8], refs[8], refs[9]
    gather_pieces(info, mine, other, total)
    first = dot_wide(total[0:16, :], weight_self[...])
    out[...] = first + dot_wide(total[16:32, :], weight_neigh[...])


def prompt(info, weight_self, weight_neigh, mine, other):
    return pl.pallas_call(
        prompt_kernel,
        in_specs=[SMEM] + [VMEM] * 10,
        out_specs=VMEM,
        out_shape=jax.ShapeDtypeStruct((PROMPTS, 1024), jnp.float32),
        scratch_shapes=[pltpu.VMEM((2 * PROMPTS, 1024), jnp.float32)],
        compiler_params=pltpu.CompilerParams(vmem_limit_bytes=24 * 2**20),
        name="prompt",
    )(info, weight_self, weight_neigh, *mine, *other)


def shards(grad_out, w_self, w_neigh, adj_tiles, tile_index, tile_count, prompt_ids):
    row, rep = lax.axis_index("rows"), lax.axis_index("rep")
    x, z, y = row % NX, (row // NX) % NZ, row // (NX * NZ)
    u = jnp.where(rep == 0, x, y)
    v = jnp.where(rep == 0, y, x)
    info = jnp.stack([rep, tile_count[0], u, v]).astype(jnp.int32)
    adj = adj_tiles[0]

    meta = jnp.zeros((16, 256), jnp.bfloat16)
    meta = meta.at[0, 0:64].set(tile_index[0].astype(jnp.bfloat16))
    meta = meta.at[1, 0:128].set(prompt_ids.astype(jnp.bfloat16))
    shares = split(info, grad_out, meta)
    packed = [shares[0]] + [send(shares[s], "u", s) for s in range(1, GROUP)]
    own = jnp.concatenate([p[0:64] for p in packed], axis=0)

    first, second = pack(adj, info, 0), pack(adj, info, 16)
    first_m, second_m = send(first, "u", 1), send(second, "u", 1)
    first_p, second_p = send(first, "u", -1), send(second, "u", -1)
    first_2, second_2 = send(first_m, "u", 1), send(second_p, "u", -1)
    tiles = [first, second, first_m, second_m, first_2, second_2, first_p, second_p]

    ups, downs = [own], [own]
    for _ in range(3):
        ups.append(send(ups[-1], "z", 1))
        downs.append(send(downs[-1], "z", -1))
    far_up = send(ups[3][0:128], "z", 1)
    far_down = send(downs[3][128:256], "z", -1)
    near = jnp.concatenate([own, ups[1], downs[1], ups[2]], axis=0)
    rest = jnp.concatenate([downs[2], ups[3], downs[3], far_up, far_down], axis=0)
    near_m, rest_m = send(near, "v", 1), send(rest, "v", 1)
    near_p, rest_p = send(near, "v", -1), send(rest, "v", -1)
    near_2, rest_2 = send(near_m, "v", 1), send(rest_p, "v", -1)
    chunks = [near, rest, near_m, rest_m, near_2, rest_2, near_p, rest_p]
    chunks = [c.reshape(16, 64, 256) for c in chunks]

    index = jnp.stack([p[64, 0:64] for p in packed]).astype(jnp.int32)
    ids = jnp.stack([p[65, 0:128] for p in packed]).astype(jnp.int32)
    sx, sz, sy = index % NX, (index // NX) % NZ, index // (NX * NZ)
    du = (u - jnp.where(rep == 0, sx, sy)) % GROUP
    dv = (v - jnp.where(rep == 0, sy, sx)) % GROUP
    dz = (z - sz) % NZ
    places = (0, 1, 3, 5, 7, 6, 4, 2)
    place = sum(jnp.where(dz == i, p, 0) for i, p in enumerate(places))
    where = dv * 32 + place * 4 + du
    where = jnp.concatenate([where, jnp.broadcast_to(rep, (1, 64)).astype(jnp.int32)])

    *parts, sums = aggregate(where, ids, tiles, chunks)

    self_term = lax.dot_general(
        grad_out, w_self, (((1,), (1,)), ((), ())), preferred_element_type=jnp.float32
    )
    weight_self, weight_neigh = w_self.T, w_neigh.T

    mine = [
        parts[0],
        send(parts[1], "u", -1),
        send(parts[3], "u", 1),
        send(parts[2], "u", 2),
    ]
    other = [send(m, "rep", 0) for m in mine]
    input_grad = finish(info, self_term, weight_neigh, mine, other)

    sums = sums + send(sums, "v", 1) + send(sums, "v", -1) + send(sums, "v", 2)
    sums = sum([send(sums, "z", s) for s in range(1, NZ)], sums)
    mine = [sums, send(sums, "u", -1), send(sums, "u", 1), send(sums, "u", 2)]
    other = [send(m, "rep", 0) for m in mine]
    prompt_grad = prompt(info, weight_self, weight_neigh, mine, other)
    return input_grad, prompt_grad


def solution(mesh):
    placed = (
        P("rows", None),
        P(),
        P(),
        P("rows", None, None, None),
        P("rows", None),
        P("rows"),
        P("rows"),
    )
    return jax.shard_map(
        shards, mesh=mesh, in_specs=placed, out_specs=(P("rows", None), P()), check_vma=False
    )
```

```python
import jax
import jax.numpy as jnp
from jax import lax
from jax.experimental import pallas as pl
from jax.experimental.pallas import tpu as pltpu
from jax.sharding import PartitionSpec as P

PROMPTS = 16
NX, NY, NZ, NREP = 4, 4, 8, 2
GROUP = 4
NEAR, REST = 20, 12
EMPTY = 128
AXES = ("rows", "rep")
ANY = pl.BlockSpec(memory_space=pl.ANY)
VMEM = pl.BlockSpec(memory_space=pltpu.VMEM)
SMEM = pl.BlockSpec(memory_space=pltpu.SMEM)


def pairs_of(role, step):
    pairs = []
    for y in range(NY):
        for z in range(NZ):
            for x in range(NX):
                for rep in range(NREP):
                    tx, ty, tz, trep = x, y, z, rep
                    if role == "rep":
                        trep = 1 - rep
                    elif role == "z":
                        tz = (z + step) % NZ
                    elif (role == "u") == (rep == 0):
                        tx = (x + step) % NX
                    else:
                        ty = (y + step) % NY
                    source = ((y * NZ + z) * NX + x) * NREP + rep
                    target = ((ty * NZ + tz) * NX + tx) * NREP + trep
                    pairs.append((source, target))
    return pairs


def send(value, role, step):
    return lax.ppermute(value, AXES, pairs_of(role, step))


def dot(a, b):
    return jnp.dot(a, b, preferred_element_type=jnp.float32)


def place():
    row, rep = lax.axis_index("rows"), lax.axis_index("rep")
    x, y = lax.rem(row, NX), lax.div(row, NX * NZ)
    z = lax.rem(lax.div(row, NX), NZ)
    u = jnp.where(rep == 0, x, y)
    v = jnp.where(rep == 0, y, x)
    return rep, u, v, z


def pack_kernel(adj, out, tiles, packed, in_sem, out_sem):
    steps = in_sem.shape[0]
    per = 64 // steps
    loads = []
    for i in range(steps):
        part = pl.ds(i * per, per)
        loads.append(pltpu.make_async_copy(adj.at[part], tiles.at[part], in_sem.at[i]))
    for i in range(steps // 2):
        loads[i].start()
        loads[steps // 2 + i].start()
    first = lax.broadcasted_iota(jnp.int32, (128, 128), 1) < 64
    rep = place()[0]
    stores = []
    for i in range(steps // 2):
        loads[i].wait()
        loads[steps // 2 + i].wait()

        @pl.when(rep == 0)
        def _():
            for k in range(i * per, i * per + per):
                packed[k] = jnp.where(first, tiles[k], pltpu.roll(tiles[32 + k], 64, 1))

        @pl.when(rep == 1)
        def _():
            for k in range(i * per, i * per + per):
                packed[k] = jnp.where(first, pltpu.roll(tiles[k], 64, 1), tiles[32 + k])

        part = pl.ds(i * per, per)
        stores.append(pltpu.make_async_copy(packed.at[part], out.at[part], out_sem.at[i]))
        stores[i].start()
    for store in stores:
        store.wait()


def pack(adj):
    return pl.pallas_call(
        pack_kernel,
        in_specs=[ANY],
        out_specs=ANY,
        out_shape=jax.ShapeDtypeStruct((32, 128, 128), jnp.bfloat16),
        scratch_shapes=[
            pltpu.VMEM((64, 128, 128), jnp.bfloat16),
            pltpu.VMEM((32, 128, 128), jnp.bfloat16),
            pltpu.SemaphoreType.DMA((8,)),
            pltpu.SemaphoreType.DMA((4,)),
        ],
        compiler_params=pltpu.CompilerParams(vmem_limit_bytes=16 * 2**20),
        name="pack",
    )(adj)


def split_kernel(count, index, ids, grad, *outs):
    rep, u, _, _ = place()
    start = pl.multiple_of(rep * 64, 64)
    as_rows = lambda value: jnp.broadcast_to(value.astype(jnp.float32), (16, value.shape[1]))
    sources = as_rows(index[...]).astype(jnp.bfloat16)
    numbers = as_rows(ids[...]).astype(jnp.bfloat16)
    used = jnp.full((16, 64), count[0].astype(jnp.float32)).astype(jnp.bfloat16)
    for step in range(GROUP):
        outs[step][0:64, :] = grad[pl.ds(start, 64), lanes_of(u, step)]
        outs[step][64:80, 0:64] = sources
        outs[step][64:80, 64:128] = used
        outs[step][64:80, 128:256] = numbers


def split(count, index, ids, grad):
    shape = jax.ShapeDtypeStruct((80, 256), jnp.bfloat16)
    return pl.pallas_call(
        split_kernel,
        in_specs=[SMEM, VMEM, VMEM, VMEM],
        out_specs=[VMEM] * GROUP,
        out_shape=[shape] * GROUP,
        name="split",
    )(count, index, ids, grad)


def unpack_kernel(*refs):
    packed, (own, where, ids) = refs[0:GROUP], refs[GROUP:]
    rep, u, v, z = place()
    rows = []
    for s in range(GROUP):
        own[64 * s : 64 * s + 64, :] = packed[s][0:64, :]
        rows.append(packed[s][64:80, :].astype(jnp.float32)[0:1])
    rows = jnp.concatenate(rows, axis=0).astype(jnp.int32)
    ids[...] = rows[:, 128:256]
    source = rows[:, 0:128]
    sx, sz, sy = source & (NX - 1), (source >> 2) & (NZ - 1), source >> 5
    du = (u - jnp.where(rep == 0, sx, sy)) & (GROUP - 1)
    dv = (v - jnp.where(rep == 0, sy, sx)) & (GROUP - 1)
    dz = (z - sz) & (NZ - 1)
    spot = jnp.zeros_like(dz)
    for i, p in enumerate((0, 1, 3, 5, 6, 7, 4, 2)):
        spot = jnp.where(dz == i, p, spot)
    lane = lax.broadcasted_iota(jnp.int32, (GROUP, 128), 1)
    count = jnp.max(jnp.where(lane == 64, source, 0), axis=1, keepdims=True)
    where[...] = jnp.where(lane < count, dv * 32 + spot * 4 + du, EMPTY)


def unpack(packed):
    return pl.pallas_call(
        unpack_kernel,
        in_specs=[VMEM] * GROUP,
        out_specs=[VMEM] * 3,
        out_shape=[
            jax.ShapeDtypeStruct((256, 256), jnp.bfloat16),
            jax.ShapeDtypeStruct((GROUP, 128), jnp.int32),
            jax.ShapeDtypeStruct((GROUP, 128), jnp.int32),
        ],
        name="unpack",
    )(*packed)


def join_kernel(*refs):
    pieces, out = refs[:-1], refs[-1]
    for i, piece in enumerate(pieces):
        out[256 * i : 256 * i + 256, :] = piece[...]


def join(*pieces):
    return pl.pallas_call(
        join_kernel,
        in_specs=[VMEM] * len(pieces),
        out_specs=VMEM,
        out_shape=jax.ShapeDtypeStruct((256 * len(pieces), 256), jnp.bfloat16),
        name="join",
    )(*pieces)


def aggregate_kernel(where, ids, *refs):
    tiles = refs[0:5]
    chunks = refs[5:13]
    parts = refs[13:17]
    sums = refs[17]
    adj, table, adj_sem, table_sem = refs[18:]
    table_copies, adj_copies = [], []
    for i in range(8):
        length = NEAR if i % 2 == 0 else REST
        begin = i // 2 * 32 + (0 if i % 2 == 0 else NEAR)
        copy = pltpu.make_async_copy(
            chunks[i], table.at[pl.ds(begin, length)], table_sem.at[i]
        )
        copy.start()
        table_copies.append(copy)
    begin = 0
    for i in range(5):
        length = tiles[i].shape[0]
        copy = pltpu.make_async_copy(tiles[i], adj.at[pl.ds(begin, length)], adj_sem.at[i])
        copy.start()
        adj_copies.append(copy)
        begin += length
    table[EMPTY] = jnp.zeros((64, 256), jnp.bfloat16)
    for copy in table_copies:
        copy.wait()
    total = jnp.zeros((PROMPTS, 256), jnp.float32)
    own = jnp.zeros((PROMPTS, 256), jnp.float32)
    rep = place()[0]
    for d in range(GROUP):
        for i in ((0,), (1,), (2, 3), (4,))[d]:
            adj_copies[i].wait()
        acc = jnp.zeros((128, 256), jnp.float32)
        for q in range(16):
            p = 2 * q
            left = jnp.concatenate([adj[d * 32 + p], adj[d * 32 + p + 1]], axis=1)
            rows = [table[where[d, k]] for k in (p, p + 32, p + 1, p + 33)]
            acc = acc + dot(left, jnp.concatenate(rows, axis=0))
        parts[d][...] = acc
        number = lax.broadcasted_iota(jnp.int32, (PROMPTS, 128), 0)
        hot = jnp.where(ids[d : d + 1, :] == number, 1.0, 0.0).astype(jnp.bfloat16)
        high = acc.astype(jnp.bfloat16)
        low = (acc - high.astype(jnp.float32)).astype(jnp.bfloat16)
        total = total + dot(hot, high) + dot(hot, low)
        row = lax.broadcasted_iota(jnp.int32, (128, 1), 0)
        mine = (row // 64) == rep
        block = jnp.concatenate([table[d], table[d]], axis=0)
        block = jnp.where(mine, block.astype(jnp.float32), 0.0).astype(jnp.bfloat16)
        own = own + dot(hot, block)
    sums[0:PROMPTS, :] = own
    sums[PROMPTS : 2 * PROMPTS, :] = total


def aggregate(where, ids, tiles, chunks):
    part = jax.ShapeDtypeStruct((128, 256), jnp.float32)
    return pl.pallas_call(
        aggregate_kernel,
        in_specs=[SMEM, VMEM] + [ANY] * 13,
        out_specs=[VMEM] * 5,
        out_shape=[part] * 4 + [jax.ShapeDtypeStruct((2 * PROMPTS, 256), jnp.float32)],
        scratch_shapes=[
            pltpu.VMEM((128, 128, 128), jnp.bfloat16),
            pltpu.VMEM((EMPTY + 1, 64, 256), jnp.bfloat16),
            pltpu.SemaphoreType.DMA((5,)),
            pltpu.SemaphoreType.DMA((8,)),
        ],
        compiler_params=pltpu.CompilerParams(vmem_limit_bytes=24 * 2**20),
        name="aggregate",
    )(where, ids, *tiles, *chunks)


def lanes_of(u, step):
    piece = lax.rem(u + step, GROUP)
    return pl.ds(pl.multiple_of(piece * 256, 256), 256)


ORDER = (0, 1, 3, 2)


def gather_pieces(groups, total, sem):
    _, u, v, _ = place()
    copies = []
    for j, pieces in enumerate(groups):
        for i, step in enumerate(ORDER):
            target = total.at[j, :, lanes_of((u, v)[j], step)]
            copies.append(pltpu.make_async_copy(pieces[i], target, sem.at[j, i]))
    for copy in copies:
        copy.start()
    for copy in copies:
        copy.wait()


def dot_t(a, b):
    return lax.dot_general(a, b, (((1,), (1,)), ((), ())), preferred_element_type=jnp.float32)


def finish_kernel(self_term, weight, *refs):
    mine, other, out, total, sem = refs[0:4], refs[4:8], refs[8], refs[9], refs[10]
    gather_pieces((mine, other), total, sem)
    neighbours = (total[0] + total[1]).astype(jnp.bfloat16)
    out[...] = (self_term[...] + dot_t(neighbours, weight[...])).astype(jnp.bfloat16)


def finish(self_term, weight, mine, other):
    return pl.pallas_call(
        finish_kernel,
        in_specs=[VMEM] * 2 + [ANY] * 8,
        out_specs=VMEM,
        out_shape=jax.ShapeDtypeStruct((128, 1024), jnp.bfloat16),
        scratch_shapes=[
            pltpu.VMEM((2, 128, 1024), jnp.float32),
            pltpu.SemaphoreType.DMA((2, GROUP)),
        ],
        compiler_params=pltpu.CompilerParams(vmem_limit_bytes=24 * 2**20),
        name="finish",
    )(self_term, weight, *mine, *other)


def dot_wide(a, b):
    high = a.astype(jnp.bfloat16)
    rest = a - high.astype(jnp.float32)
    middle = rest.astype(jnp.bfloat16)
    low = (rest - middle.astype(jnp.float32)).astype(jnp.bfloat16)
    product = dot_t(jnp.concatenate([high, middle, low], axis=0), b)
    return product[0:16] + product[16:32] + product[32:48]


def prompt_kernel(weight_self, weight_neigh, *refs):
    mine, out, total, sem = refs[0:4], refs[4], refs[5], refs[6]
    gather_pieces((mine,), total, sem)
    sums = total[0]
    first = dot_wide(sums[0:16, :], weight_self[...])
    out[...] = first + dot_wide(sums[16:32, :], weight_neigh[...])


def prompt(weight_self, weight_neigh, mine):
    return pl.pallas_call(
        prompt_kernel,
        in_specs=[VMEM] * 2 + [ANY] * 4,
        out_specs=VMEM,
        out_shape=jax.ShapeDtypeStruct((PROMPTS, 1024), jnp.float32),
        scratch_shapes=[
            pltpu.VMEM((1, 2 * PROMPTS, 1024), jnp.float32),
            pltpu.SemaphoreType.DMA((1, GROUP)),
        ],
        compiler_params=pltpu.CompilerParams(vmem_limit_bytes=24 * 2**20),
        name="prompt",
    )(weight_self, weight_neigh, *mine)


def total_of_four(value, role):
    near = send(value, role, 1), send(value, role, -1)
    return (value + send(value, role, 2)) + (near[0] + near[1])


def shards(grad_out, w_self, w_neigh, adj_tiles, tile_index, tile_count, prompt_ids):
    shares = split(tile_count, tile_index, prompt_ids[None, :], grad_out)
    packed = [shares[0]] + [send(shares[s], "u", s) for s in range(1, GROUP)]
    mine = pack(adj_tiles[0])
    mine, packed = lax.optimization_barrier((mine, packed))
    own, where, ids = unpack(packed)
    left, right = send(mine, "u", 1), send(mine, "u", -1)

    z1, z7, z2, z6 = [send(own, "z", s) for s in (1, -1, 2, -2)]
    z3, z4, z5 = send(z2, "z", 1), send(z2, "z", 2), send(z6, "z", -1)

    near = join(own, z1, z7, z2, z6)
    near_m, near_p = send(near, "v", 1), send(near, "v", -1)
    far = [send(left[0:16], "u", 1), send(right[16:32], "u", -1)]
    tiles = [mine, left, *far, right]
    rest = join(z3, z4, z5)
    self_term, rest = lax.optimization_barrier((dot_t(grad_out, w_self), rest))
    rest_m, rest_p = send(rest, "v", 1), send(rest, "v", -1)
    near_2, rest_2 = send(near_m, "v", 1), send(rest_p, "v", -1)
    chunks = [near, rest, near_m, rest_m, near_2, rest_2, near_p, rest_p]
    chunks = [c.reshape(c.shape[0] // 64, 64, 256) for c in chunks]

    *parts, sums = aggregate(where, ids, tiles, chunks)

    owned = [
        parts[0],
        send(parts[1], "u", -1),
        send(parts[3], "u", 1),
        send(parts[2], "u", 2),
    ]

    sums = total_of_four(sums, "v")
    sums = sums + send(sums, "z", 4)
    sums = total_of_four(sums, "z")
    pieces = [sums, send(sums, "u", -1), send(sums, "u", 1), send(sums, "u", 2)]
    owned, pieces = lax.optimization_barrier((owned, pieces))
    product = prompt(w_self, w_neigh, pieces)
    prompt_grad = product + send(product, "rep", 0)
    other = [send(m, "rep", 0) for m in owned]
    input_grad = finish(self_term, w_neigh, owned, other)
    return input_grad, prompt_grad


def solution(mesh):
    placed = (
        P("rows", None),
        P(),
        P(),
        P("rows", None, None, None),
        P("rows", None),
        P("rows"),
        P("rows"),
    )
    return jax.shard_map(
        shards, mesh=mesh, in_specs=placed, out_specs=(P("rows", None), P()), check_vma=False
    )
```

```python
import jax
import jax.numpy as jnp
from jax import lax
from jax.experimental import pallas as pl
from jax.experimental.pallas import tpu as pltpu
from jax.sharding import PartitionSpec as P

PROMPTS = 16
NX, NY, NZ, NREP = 4, 4, 8, 2
GROUP = 4
NEAR, REST = 20, 12
EMPTY = 128
AXES = ("rows", "rep")
ANY = pl.BlockSpec(memory_space=pl.ANY)
VMEM = pl.BlockSpec(memory_space=pltpu.VMEM)
SMEM = pl.BlockSpec(memory_space=pltpu.SMEM)


def pairs_of(role, step):
    pairs = []
    for y in range(NY):
        for z in range(NZ):
            for x in range(NX):
                for rep in range(NREP):
                    tx, ty, tz, trep = x, y, z, rep
                    if role == "rep":
                        trep = 1 - rep
                    elif role == "z":
                        tz = (z + step) % NZ
                    elif (role == "u") == (rep == 0):
                        tx = (x + step) % NX
                    else:
                        ty = (y + step) % NY
                    source = ((y * NZ + z) * NX + x) * NREP + rep
                    target = ((ty * NZ + tz) * NX + tx) * NREP + trep
                    pairs.append((source, target))
    return pairs


def send(value, role, step):
    return lax.ppermute(value, AXES, pairs_of(role, step))


def dot(a, b):
    return jnp.dot(a, b, preferred_element_type=jnp.float32)


def place():
    row, rep = lax.axis_index("rows"), lax.axis_index("rep")
    x, y = lax.rem(row, NX), lax.div(row, NX * NZ)
    z = lax.rem(lax.div(row, NX), NZ)
    u = jnp.where(rep == 0, x, y)
    v = jnp.where(rep == 0, y, x)
    return rep, u, v, z


def pack_kernel(adj, out, tiles, packed, in_sem, out_sem):
    steps = in_sem.shape[0]
    per = 64 // steps
    loads = []
    for i in range(steps):
        part = pl.ds(i * per, per)
        loads.append(pltpu.make_async_copy(adj.at[part], tiles.at[part], in_sem.at[i]))
    for i in range(steps // 2):
        loads[i].start()
        loads[steps // 2 + i].start()
    first = lax.broadcasted_iota(jnp.int32, (128, 128), 1) < 64
    rep = place()[0]
    stores = []
    for i in range(steps // 2):
        loads[i].wait()
        loads[steps // 2 + i].wait()

        @pl.when(rep == 0)
        def _():
            for k in range(i * per, i * per + per):
                packed[k] = jnp.where(first, tiles[k], pltpu.roll(tiles[32 + k], 64, 1))

        @pl.when(rep == 1)
        def _():
            for k in range(i * per, i * per + per):
                packed[k] = jnp.where(first, pltpu.roll(tiles[k], 64, 1), tiles[32 + k])

        part = pl.ds(i * per, per)
        stores.append(pltpu.make_async_copy(packed.at[part], out.at[part], out_sem.at[i]))
        stores[i].start()
    for store in stores:
        store.wait()


def pack(adj):
    return pl.pallas_call(
        pack_kernel,
        in_specs=[ANY],
        out_specs=ANY,
        out_shape=jax.ShapeDtypeStruct((32, 128, 128), jnp.bfloat16),
        scratch_shapes=[
            pltpu.VMEM((64, 128, 128), jnp.bfloat16),
            pltpu.VMEM((32, 128, 128), jnp.bfloat16),
            pltpu.SemaphoreType.DMA((8,)),
            pltpu.SemaphoreType.DMA((4,)),
        ],
        compiler_params=pltpu.CompilerParams(vmem_limit_bytes=16 * 2**20),
        name="pack",
    )(adj)


def split_kernel(count, index, ids, grad, *outs):
    rep, u, _, _ = place()
    start = pl.multiple_of(rep * 64, 64)
    as_rows = lambda value: jnp.broadcast_to(value.astype(jnp.float32), (16, value.shape[1]))
    sources = as_rows(index[...]).astype(jnp.bfloat16)
    numbers = as_rows(ids[...]).astype(jnp.bfloat16)
    used = jnp.full((16, 64), count[0].astype(jnp.float32)).astype(jnp.bfloat16)
    for step in range(GROUP):
        outs[step][0:64, :] = grad[pl.ds(start, 64), lanes_of(u, step)]
        outs[step][64:80, 0:64] = sources
        outs[step][64:80, 64:128] = used
        outs[step][64:80, 128:256] = numbers


def split(count, index, ids, grad):
    shape = jax.ShapeDtypeStruct((80, 256), jnp.bfloat16)
    return pl.pallas_call(
        split_kernel,
        in_specs=[SMEM, VMEM, VMEM, VMEM],
        out_specs=[VMEM] * GROUP,
        out_shape=[shape] * GROUP,
        name="split",
    )(count, index, ids, grad)


def aggregate_kernel(where, ids, *refs):
    tiles = refs[0:5]
    chunks = refs[5:13]
    parts = refs[13:17]
    sums = refs[17]
    adj, table, adj_sem, table_sem = refs[18:]
    table_copies, adj_copies = [], []
    for i in range(8):
        length = NEAR if i % 2 == 0 else REST
        begin = i // 2 * 32 + (0 if i % 2 == 0 else NEAR)
        copy = pltpu.make_async_copy(
            chunks[i], table.at[pl.ds(begin, length)], table_sem.at[i]
        )
        copy.start()
        table_copies.append(copy)
    begin = 0
    for i in range(5):
        length = tiles[i].shape[0]
        copy = pltpu.make_async_copy(tiles[i], adj.at[pl.ds(begin, length)], adj_sem.at[i])
        copy.start()
        adj_copies.append(copy)
        begin += length
    table[EMPTY] = jnp.zeros((64, 256), jnp.bfloat16)
    for copy in table_copies:
        copy.wait()
    total = jnp.zeros((PROMPTS, 256), jnp.float32)
    own = jnp.zeros((PROMPTS, 256), jnp.float32)
    rep = place()[0]
    for d in range(GROUP):
        for i in ((0,), (1,), (2, 3), (4,))[d]:
            adj_copies[i].wait()
        acc = jnp.zeros((128, 256), jnp.float32)
        for q in range(16):
            p = 2 * q
            left = jnp.concatenate([adj[d * 32 + p], adj[d * 32 + p + 1]], axis=1)
            rows = [table[where[d, k]] for k in (p, p + 32, p + 1, p + 33)]
            acc = acc + dot(left, jnp.concatenate(rows, axis=0))
        parts[d][...] = acc
        number = lax.broadcasted_iota(jnp.int32, (PROMPTS, 128), 0)
        hot = jnp.where(ids[d : d + 1, :] == number, 1.0, 0.0).astype(jnp.bfloat16)
        high = acc.astype(jnp.bfloat16)
        low = (acc - high.astype(jnp.float32)).astype(jnp.bfloat16)
        total = total + dot(hot, high) + dot(hot, low)
        row = lax.broadcasted_iota(jnp.int32, (128, 1), 0)
        mine = (row // 64) == rep
        block = jnp.concatenate([table[d], table[d]], axis=0)
        block = jnp.where(mine, block.astype(jnp.float32), 0.0).astype(jnp.bfloat16)
        own = own + dot(hot, block)
    sums[0:PROMPTS, :] = own
    sums[PROMPTS : 2 * PROMPTS, :] = total


def aggregate(where, ids, tiles, chunks):
    part = jax.ShapeDtypeStruct((128, 256), jnp.float32)
    return pl.pallas_call(
        aggregate_kernel,
        in_specs=[SMEM, VMEM] + [ANY] * 13,
        out_specs=[VMEM] * 5,
        out_shape=[part] * 4 + [jax.ShapeDtypeStruct((2 * PROMPTS, 256), jnp.float32)],
        scratch_shapes=[
            pltpu.VMEM((128, 128, 128), jnp.bfloat16),
            pltpu.VMEM((EMPTY + 1, 64, 256), jnp.bfloat16),
            pltpu.SemaphoreType.DMA((5,)),
            pltpu.SemaphoreType.DMA((8,)),
        ],
        compiler_params=pltpu.CompilerParams(vmem_limit_bytes=24 * 2**20),
        name="aggregate",
    )(where, ids, *tiles, *chunks)


def lanes_of(u, step):
    piece = lax.rem(u + step, GROUP)
    return pl.ds(pl.multiple_of(piece * 256, 256), 256)


ORDER = (0, 1, 3, 2)


def gather_pieces(groups, total, sem):
    _, u, v, _ = place()
    copies = []
    for j, pieces in enumerate(groups):
        for i, step in enumerate(ORDER):
            target = total.at[j, :, lanes_of((u, v)[j], step)]
            copies.append(pltpu.make_async_copy(pieces[i], target, sem.at[j, i]))
    for copy in copies:
        copy.start()
    for copy in copies:
        copy.wait()


def dot_t(a, b):
    return lax.dot_general(a, b, (((1,), (1,)), ((), ())), preferred_element_type=jnp.float32)


def finish_kernel(self_term, weight, *refs):
    mine, other, out, total, sem = refs[0:4], refs[4:8], refs[8], refs[9], refs[10]
    gather_pieces((mine, other), total, sem)
    neighbours = (total[0] + total[1]).astype(jnp.bfloat16)
    out[...] = (self_term[...] + dot_t(neighbours, weight[...])).astype(jnp.bfloat16)


def finish(self_term, weight, mine, other):
    return pl.pallas_call(
        finish_kernel,
        in_specs=[VMEM] * 2 + [ANY] * 8,
        out_specs=VMEM,
        out_shape=jax.ShapeDtypeStruct((128, 1024), jnp.bfloat16),
        scratch_shapes=[
            pltpu.VMEM((2, 128, 1024), jnp.float32),
            pltpu.SemaphoreType.DMA((2, GROUP)),
        ],
        compiler_params=pltpu.CompilerParams(vmem_limit_bytes=24 * 2**20),
        name="finish",
    )(self_term, weight, *mine, *other)


def dot_wide(a, b):
    high = a.astype(jnp.bfloat16)
    rest = a - high.astype(jnp.float32)
    middle = rest.astype(jnp.bfloat16)
    low = (rest - middle.astype(jnp.float32)).astype(jnp.bfloat16)
    product = dot_t(jnp.concatenate([high, middle, low], axis=0), b)
    return product[0:16] + product[16:32] + product[32:48]


def prompt_kernel(weight_self, weight_neigh, *refs):
    mine, out, total, sem = refs[0:4], refs[4], refs[5], refs[6]
    gather_pieces((mine,), total, sem)
    sums = total[0]
    first = dot_wide(sums[0:16, :], weight_self[...])
    out[...] = first + dot_wide(sums[16:32, :], weight_neigh[...])


def prompt(weight_self, weight_neigh, mine):
    return pl.pallas_call(
        prompt_kernel,
        in_specs=[VMEM] * 2 + [ANY] * 4,
        out_specs=VMEM,
        out_shape=jax.ShapeDtypeStruct((PROMPTS, 1024), jnp.float32),
        scratch_shapes=[
            pltpu.VMEM((1, 2 * PROMPTS, 1024), jnp.float32),
            pltpu.SemaphoreType.DMA((1, GROUP)),
        ],
        compiler_params=pltpu.CompilerParams(vmem_limit_bytes=24 * 2**20),
        name="prompt",
    )(weight_self, weight_neigh, *mine)


def total_of_four(value, role, step=1):
    near = send(value, role, step), send(value, role, -step)
    return (value + send(value, role, 2 * step)) + (near[0] + near[1])


def shards(grad_out, w_self, w_neigh, adj_tiles, tile_index, tile_count, prompt_ids):
    shares = split(tile_count, tile_index, prompt_ids[None, :], grad_out)
    packed = [shares[0]] + [send(shares[s], "u", s) for s in range(1, GROUP)]
    own = jnp.concatenate([p[0:64] for p in packed], axis=0)

    mine = pack(adj_tiles[0])
    left, right = send(mine, "u", 1), send(mine, "u", -1)

    z1, z7, z2, z6 = [send(own, "z", s) for s in (1, -1, 2, -2)]
    z3, z4, z5 = send(z2, "z", 1), send(z2, "z", 2), send(z6, "z", -1)

    near = jnp.concatenate([own, z1, z7, z2, z6], axis=0)
    near_m, near_p = send(near, "v", 1), send(near, "v", -1)
    far = [send(left[0:16], "u", 1), send(right[16:32], "u", -1)]
    tiles = [mine, left, *far, right]
    rest = jnp.concatenate([z3, z4, z5], axis=0)
    self_term, rest = lax.optimization_barrier((dot_t(grad_out, w_self), rest))
    rest_m, rest_p = send(rest, "v", 1), send(rest, "v", -1)
    near_2, rest_2 = send(near_m, "v", 1), send(rest_p, "v", -1)
    chunks = [near, rest, near_m, rest_m, near_2, rest_2, near_p, rest_p]
    chunks = [c.reshape(c.shape[0] // 64, 64, 256) for c in chunks]

    rep, u, v, z = place()
    index = jnp.stack([p[64, 0:64] for p in packed]).astype(jnp.int32)
    count = jnp.stack([p[64, 64:128] for p in packed]).astype(jnp.int32)
    ids = jnp.stack([p[64, 128:256] for p in packed]).astype(jnp.int32)
    sx, sz, sy = index % NX, (index // NX) % NZ, index // (NX * NZ)
    du = (u - jnp.where(rep == 0, sx, sy)) % GROUP
    dv = (v - jnp.where(rep == 0, sy, sx)) % GROUP
    dz = (z - sz) % NZ
    spot = sum(jnp.where(dz == i, p, 0) for i, p in enumerate((0, 1, 3, 5, 6, 7, 4, 2)))
    where = jnp.where(jnp.arange(64)[None, :] < count, dv * 32 + spot * 4 + du, EMPTY)
    where = where.astype(jnp.int32)

    *parts, sums = aggregate(where, ids, tiles, chunks)

    owned = [
        parts[0],
        send(parts[1], "u", -1),
        send(parts[3], "u", 1),
        send(parts[2], "u", 2),
    ]

    sums = total_of_four(sums, "v")
    sums = total_of_four(sums, "z", 2)
    sums = sums + send(sums, "z", 1)
    pieces = [sums, send(sums, "u", -1), send(sums, "u", 1), send(sums, "u", 2)]
    owned, pieces = lax.optimization_barrier((owned, pieces))
    product = prompt(w_self, w_neigh, pieces)
    prompt_grad = product + send(product, "rep", 0)
    other = [send(m, "rep", 0) for m in owned]
    input_grad = finish(self_term, w_neigh, owned, other)
    return input_grad, prompt_grad


def solution(mesh):
    placed = (
        P("rows", None),
        P(),
        P(),
        P("rows", None, None, None),
        P("rows", None),
        P("rows"),
        P("rows"),
    )
    return jax.shard_map(
        shards, mesh=mesh, in_specs=placed, out_specs=(P("rows", None), P()), check_vma=False
    )
```

```python
import jax
import jax.numpy as jnp
from jax import lax
from jax.experimental import pallas as pl
from jax.experimental.pallas import tpu as pltpu
from jax.sharding import PartitionSpec as P

PROMPTS = 16
NX, NY, NZ, NREP = 4, 4, 8, 2
GROUP = 4
NEAR, REST = 20, 12
EMPTY = 128
AXES = ("rows", "rep")
ANY = pl.BlockSpec(memory_space=pl.ANY)
VMEM = pl.BlockSpec(memory_space=pltpu.VMEM)
SMEM = pl.BlockSpec(memory_space=pltpu.SMEM)


def pairs_of(role, step):
    pairs = []
    for y in range(NY):
        for z in range(NZ):
            for x in range(NX):
                for rep in range(NREP):
                    tx, ty, tz, trep = x, y, z, rep
                    if role == "rep":
                        trep = 1 - rep
                    elif role == "z":
                        tz = (z + step) % NZ
                    elif (role == "u") == (rep == 0):
                        tx = (x + step) % NX
                    else:
                        ty = (y + step) % NY
                    source = ((y * NZ + z) * NX + x) * NREP + rep
                    target = ((ty * NZ + tz) * NX + tx) * NREP + trep
                    pairs.append((source, target))
    return pairs


def send(value, role, step):
    return lax.ppermute(value, AXES, pairs_of(role, step))


def dot(a, b):
    return jnp.dot(a, b, preferred_element_type=jnp.float32)


def place():
    row, rep = lax.axis_index("rows"), lax.axis_index("rep")
    x, y = lax.rem(row, NX), lax.div(row, NX * NZ)
    z = lax.rem(lax.div(row, NX), NZ)
    u = jnp.where(rep == 0, x, y)
    v = jnp.where(rep == 0, y, x)
    return rep, u, v, z


def pack_kernel(adj, out, tiles, packed, in_sem, out_sem):
    steps = in_sem.shape[0]
    per = 64 // steps
    loads = []
    for i in range(steps):
        part = pl.ds(i * per, per)
        loads.append(pltpu.make_async_copy(adj.at[part], tiles.at[part], in_sem.at[i]))
    for i in range(steps // 2):
        loads[i].start()
        loads[steps // 2 + i].start()
    first = lax.broadcasted_iota(jnp.int32, (128, 128), 1) < 64
    rep = place()[0]
    stores = []
    for i in range(steps // 2):
        loads[i].wait()
        loads[steps // 2 + i].wait()

        @pl.when(rep == 0)
        def _():
            for k in range(i * per, i * per + per):
                packed[k] = jnp.where(first, tiles[k], pltpu.roll(tiles[32 + k], 64, 1))

        @pl.when(rep == 1)
        def _():
            for k in range(i * per, i * per + per):
                packed[k] = jnp.where(first, pltpu.roll(tiles[k], 64, 1), tiles[32 + k])

        part = pl.ds(i * per, per)
        stores.append(pltpu.make_async_copy(packed.at[part], out.at[part], out_sem.at[i]))
        stores[i].start()
    for store in stores:
        store.wait()


def pack(adj):
    return pl.pallas_call(
        pack_kernel,
        in_specs=[ANY],
        out_specs=ANY,
        out_shape=jax.ShapeDtypeStruct((32, 128, 128), jnp.bfloat16),
        scratch_shapes=[
            pltpu.VMEM((64, 128, 128), jnp.bfloat16),
            pltpu.VMEM((32, 128, 128), jnp.bfloat16),
            pltpu.SemaphoreType.DMA((8,)),
            pltpu.SemaphoreType.DMA((4,)),
        ],
        compiler_params=pltpu.CompilerParams(vmem_limit_bytes=16 * 2**20),
        name="pack",
    )(adj)


def split_kernel(count, index, ids, grad, *outs):
    rep, u, _, _ = place()
    start = pl.multiple_of(rep * 64, 64)
    as_rows = lambda value: jnp.broadcast_to(value.astype(jnp.float32), (16, value.shape[1]))
    sources = as_rows(index[...]).astype(jnp.bfloat16)
    numbers = as_rows(ids[...]).astype(jnp.bfloat16)
    used = jnp.full((16, 64), count[0].astype(jnp.float32)).astype(jnp.bfloat16)
    for step in range(GROUP):
        outs[step][0:64, :] = grad[pl.ds(start, 64), lanes_of(u, step)]
        outs[step][64:80, 0:64] = sources
        outs[step][64:80, 64:128] = used
        outs[step][64:80, 128:256] = numbers


def split(count, index, ids, grad):
    shape = jax.ShapeDtypeStruct((80, 256), jnp.bfloat16)
    return pl.pallas_call(
        split_kernel,
        in_specs=[SMEM, VMEM, VMEM, VMEM],
        out_specs=[VMEM] * GROUP,
        out_shape=[shape] * GROUP,
        name="split",
    )(count, index, ids, grad)


def aggregate_kernel(where, ids, *refs):
    tiles = refs[0:5]
    chunks = refs[5:13]
    parts = refs[13:17]
    sums = refs[17]
    adj, table, adj_sem, table_sem = refs[18:]
    table_copies, adj_copies = [], []
    for i in range(8):
        length = NEAR if i % 2 == 0 else REST
        begin = i // 2 * 32 + (0 if i % 2 == 0 else NEAR)
        copy = pltpu.make_async_copy(
            chunks[i], table.at[pl.ds(begin, length)], table_sem.at[i]
        )
        copy.start()
        table_copies.append(copy)
    begin = 0
    for i in range(5):
        length = tiles[i].shape[0]
        copy = pltpu.make_async_copy(tiles[i], adj.at[pl.ds(begin, length)], adj_sem.at[i])
        copy.start()
        adj_copies.append(copy)
        begin += length
    table[EMPTY] = jnp.zeros((64, 256), jnp.bfloat16)
    for copy in table_copies:
        copy.wait()
    total = jnp.zeros((PROMPTS, 256), jnp.float32)
    own = jnp.zeros((PROMPTS, 256), jnp.float32)
    rep = place()[0]
    for d in range(GROUP):
        for i in ((0,), (1,), (2, 3), (4,))[d]:
            adj_copies[i].wait()
        acc = jnp.zeros((128, 256), jnp.float32)
        for q in range(16):
            p = 2 * q
            left = jnp.concatenate([adj[d * 32 + p], adj[d * 32 + p + 1]], axis=1)
            rows = [table[where[d, k]] for k in (p, p + 32, p + 1, p + 33)]
            acc = acc + dot(left, jnp.concatenate(rows, axis=0))
        parts[d][...] = acc
        number = lax.broadcasted_iota(jnp.int32, (PROMPTS, 128), 0)
        hot = jnp.where(ids[d : d + 1, :] == number, 1.0, 0.0).astype(jnp.bfloat16)
        high = acc.astype(jnp.bfloat16)
        low = (acc - high.astype(jnp.float32)).astype(jnp.bfloat16)
        total = total + dot(hot, high) + dot(hot, low)
        row = lax.broadcasted_iota(jnp.int32, (128, 1), 0)
        mine = (row // 64) == rep
        block = jnp.concatenate([table[d], table[d]], axis=0)
        block = jnp.where(mine, block.astype(jnp.float32), 0.0).astype(jnp.bfloat16)
        own = own + dot(hot, block)
    sums[0:PROMPTS, :] = own
    sums[PROMPTS : 2 * PROMPTS, :] = total


def aggregate(where, ids, tiles, chunks):
    part = jax.ShapeDtypeStruct((128, 256), jnp.float32)
    return pl.pallas_call(
        aggregate_kernel,
        in_specs=[SMEM, VMEM] + [ANY] * 13,
        out_specs=[VMEM] * 5,
        out_shape=[part] * 4 + [jax.ShapeDtypeStruct((2 * PROMPTS, 256), jnp.float32)],
        scratch_shapes=[
            pltpu.VMEM((128, 128, 128), jnp.bfloat16),
            pltpu.VMEM((EMPTY + 1, 64, 256), jnp.bfloat16),
            pltpu.SemaphoreType.DMA((5,)),
            pltpu.SemaphoreType.DMA((8,)),
        ],
        compiler_params=pltpu.CompilerParams(vmem_limit_bytes=24 * 2**20),
        name="aggregate",
    )(where, ids, *tiles, *chunks)


def lanes_of(u, step):
    piece = lax.rem(u + step, GROUP)
    return pl.ds(pl.multiple_of(piece * 256, 256), 256)


ORDER = (0, 1, 3, 2)


def gather_pieces(groups, total, sem):
    _, u, v, _ = place()
    copies = []
    for j, pieces in enumerate(groups):
        for i, step in enumerate(ORDER):
            target = total.at[j, :, lanes_of((u, v)[j], step)]
            copies.append(pltpu.make_async_copy(pieces[i], target, sem.at[j, i]))
    for copy in copies:
        copy.start()
    for copy in copies:
        copy.wait()


def dot_t(a, b):
    return lax.dot_general(a, b, (((1,), (1,)), ((), ())), preferred_element_type=jnp.float32)


def finish_kernel(self_term, weight, *refs):
    mine, other, out, total, sem = refs[0:4], refs[4:8], refs[8], refs[9], refs[10]
    gather_pieces((mine, other), total, sem)
    neighbours = (total[0] + total[1]).astype(jnp.bfloat16)
    out[...] = (self_term[...] + dot_t(neighbours, weight[...])).astype(jnp.bfloat16)


def finish(self_term, weight, mine, other):
    return pl.pallas_call(
        finish_kernel,
        in_specs=[VMEM] * 2 + [ANY] * 8,
        out_specs=VMEM,
        out_shape=jax.ShapeDtypeStruct((128, 1024), jnp.bfloat16),
        scratch_shapes=[
            pltpu.VMEM((2, 128, 1024), jnp.float32),
            pltpu.SemaphoreType.DMA((2, GROUP)),
        ],
        compiler_params=pltpu.CompilerParams(vmem_limit_bytes=24 * 2**20),
        name="finish",
    )(self_term, weight, *mine, *other)


def dot_wide(a, b):
    high = a.astype(jnp.bfloat16)
    rest = a - high.astype(jnp.float32)
    middle = rest.astype(jnp.bfloat16)
    low = (rest - middle.astype(jnp.float32)).astype(jnp.bfloat16)
    product = dot_t(jnp.concatenate([high, middle, low], axis=0), b)
    return product[0:16] + product[16:32] + product[32:48]


def prompt_kernel(weight_self, weight_neigh, *refs):
    mine, out, total, sem = refs[0:4], refs[4], refs[5], refs[6]
    gather_pieces((mine,), total, sem)
    sums = total[0]
    first = dot_wide(sums[0:16, :], weight_self[...])
    out[...] = first + dot_wide(sums[16:32, :], weight_neigh[...])


def prompt(weight_self, weight_neigh, mine):
    return pl.pallas_call(
        prompt_kernel,
        in_specs=[VMEM] * 2 + [ANY] * 4,
        out_specs=VMEM,
        out_shape=jax.ShapeDtypeStruct((PROMPTS, 1024), jnp.float32),
        scratch_shapes=[
            pltpu.VMEM((1, 2 * PROMPTS, 1024), jnp.float32),
            pltpu.SemaphoreType.DMA((1, GROUP)),
        ],
        compiler_params=pltpu.CompilerParams(vmem_limit_bytes=24 * 2**20),
        name="prompt",
    )(weight_self, weight_neigh, *mine)


def total_of_four(value, role, step=1):
    near = send(value, role, step), send(value, role, -step)
    return (value + send(value, role, 2 * step)) + (near[0] + near[1])


def shards(grad_out, w_self, w_neigh, adj_tiles, tile_index, tile_count, prompt_ids):
    shares = split(tile_count, tile_index, prompt_ids[None, :], grad_out)
    packed = [shares[0]] + [send(shares[s], "u", s) for s in range(1, GROUP)]
    own = jnp.concatenate([p[0:64] for p in packed], axis=0)

    mine = pack(adj_tiles[0])
    left, right = send(mine, "u", 1), send(mine, "u", -1)

    z1, z7, z2, z6 = [send(own, "z", s) for s in (1, -1, 2, -2)]
    z3, z4, z5 = send(z2, "z", 1), send(z2, "z", 2), send(z6, "z", -1)

    near = jnp.concatenate([own, z1, z7, z2, z6], axis=0)
    near_m, near_p = send(near, "v", 1), send(near, "v", -1)
    far = [send(left[0:16], "u", 1), send(right[16:32], "u", -1)]
    tiles = [mine, left, *far, right]
    rest = jnp.concatenate([z3, z4, z5], axis=0)
    self_term, rest = lax.optimization_barrier((dot_t(grad_out, w_self), rest))
    rest_m, rest_p = send(rest, "v", 1), send(rest, "v", -1)
    near_2, rest_2 = send(near_m, "v", 1), send(rest_p, "v", -1)
    chunks = [near, rest, near_m, rest_m, near_2, rest_2, near_p, rest_p]
    chunks = [c.reshape(c.shape[0] // 64, 64, 256) for c in chunks]

    rep, u, v, z = place()
    index = jnp.stack([p[64, 0:64] for p in packed]).astype(jnp.int32)
    count = jnp.stack([p[64, 64:128] for p in packed]).astype(jnp.int32)
    ids = jnp.stack([p[64, 128:256] for p in packed]).astype(jnp.int32)
    sx, sz, sy = index % NX, (index // NX) % NZ, index // (NX * NZ)
    du = (u - jnp.where(rep == 0, sx, sy)) % GROUP
    dv = (v - jnp.where(rep == 0, sy, sx)) % GROUP
    dz = (z - sz) % NZ
    spot = sum(jnp.where(dz == i, p, 0) for i, p in enumerate((0, 1, 3, 5, 6, 7, 4, 2)))
    where = jnp.where(jnp.arange(64)[None, :] < count, dv * 32 + spot * 4 + du, EMPTY)
    where = where.astype(jnp.int32)

    *parts, sums = aggregate(where, ids, tiles, chunks)

    owned = [
        parts[0],
        send(parts[1], "u", -1),
        send(parts[3], "u", 1),
        send(parts[2], "u", 2),
    ]

    sums = total_of_four(sums, "v")
    sums = total_of_four(sums, "z", 2)
    sums = sums + send(sums, "z", 1)
    pieces = [sums, send(sums, "u", -1), send(sums, "u", 1), send(sums, "u", 2)]
    owned, pieces = lax.optimization_barrier((owned, pieces))
    product = prompt(w_self, w_neigh, pieces)
    received = send(product, "rep", 0)
    other = [send(m, "rep", 0) for m in owned]
    input_grad = finish(self_term, w_neigh, owned, other)
    received, input_grad = lax.optimization_barrier((received, input_grad))
    return input_grad, product + received


def solution(mesh):
    placed = (
        P("rows", None),
        P(),
        P(),
        P("rows", None, None, None),
        P("rows", None),
        P("rows"),
        P("rows"),
    )
    return jax.shard_map(
        shards, mesh=mesh, in_specs=placed, out_specs=(P("rows", None), P()), check_vma=False
    )
```
